32 devices in a mesh: prow: 8 (over z, x), pcol: 4 (over y, core).
Axes of the slice: x: 2, y: 2, z: 4, core: 2. Of those that a mesh axis runs over, the one named last changes fastest.
Arguments:
- inverse_pool: float32 [1536, 1536], P('prow', 'pcol'), may hold values from -6 to 6
- panel_one: float32 [1536, 512], P(('prow', 'pcol')), may hold values from -0.1875 to 0.1875
- panel_two: float32 [1536, 512], P(('prow', 'pcol')), may hold values from -0.21875 to 0.21875
- upper_two: float32 [512, 512], replicated, may hold values from -0.25 to 0.25
- lower_one: float32 [512, 512], replicated, as said below
- lower_two: float32 [512, 512], replicated, as said below
- list_one: int32 [9], replicated, may hold values from 0 to 11, as said below
- list_two: int32 [6], replicated, may hold values from 0 to 11, as said below
Outputs:
- first_offdiag: float32 [1536, 512], P(('prow', 'pcol'))
- first_diag: float32 [512, 512], replicated
- second_offdiag: float32 [1536, 512], P(('prow', 'pcol'))
- second_coupling: float32 [512, 512], replicated
- second_diag: float32 [512, 512], replicated
The draws below stay inside these ranges and needn't reach their ends.
Inputs may be any that keep to these rules, and one draw needn't show every extreme that they name: `list_one`: distinct block numbers, among them 0, 6 and 11. `list_two`: distinct block numbers, each of which is also in list_one, among them 0, 6 and 11. `lower_one`: lower triangular with a diagonal of 1 to 1.5. `lower_two`: lower triangular with a diagonal of 1 to 1.5.
All inputs are finite; a program needn't handle non-finite values.
Results may differ from the reference program's by a relative error of at most 0.000073.
Values sent between devices are 32-bit elements; how exact they have to be, the bound alone decides.
A program may use at most 64 MiB of HBM per device.

```python
import jax
import jax.numpy as jnp
from jax import lax

W = 512
BLK = 128
NP = 1536
NBLK = 12
NSEL1 = 9
NSEL2 = 6


def lower_factor(key):
    strict = jax.random.normal(jax.random.fold_in(key, 3), (W, W), jnp.float32) * (0.6 / W ** 0.5)
    diagonal = 1.0 + 0.5 * jax.random.uniform(jax.random.fold_in(key, 4), (W,), jnp.float32)
    return jnp.tril(strict, -1) + jnp.diag(diagonal)


def draw_lower_one(key, part):
    return lower_factor(jax.random.fold_in(key, 21))


def draw_lower_two(key, part):
    return lower_factor(jax.random.fold_in(key, 22))


def ancestor_order(key):
    shuffled = jax.random.permutation(jax.random.fold_in(key, 11), NBLK).astype(jnp.int32)
    blocks = jnp.arange(NBLK, dtype=jnp.int32)
    middle = NP // 2 // BLK
    scores = shuffled + 3
    scores = jnp.where(blocks == 0, 0, scores)
    scores = jnp.where(blocks == middle, 1, scores)
    scores = jnp.where(blocks == NBLK - 1, 2, scores)
    return jnp.argsort(scores, stable=True).astype(jnp.int32)


def draw_list_one(key, part):
    chosen = ancestor_order(key)[:NSEL1]
    return jax.random.permutation(jax.random.fold_in(key, 13), chosen).astype(jnp.int32)


def draw_list_two(key, part):
    chosen = ancestor_order(key)[:NSEL2]
    return jax.random.permutation(jax.random.fold_in(key, 12), chosen).astype(jnp.int32)


def block_levels(rng, shape, split, low, top_value):
    def one(dim, parts):
        draws = jax.random.uniform(jax.random.fold_in(jax.random.fold_in(rng, 6), dim), (parts,), jnp.float32, low / len(split), top_value / len(split))
        return jnp.repeat(jnp.exp(draws), shape[dim] // parts).reshape((-1,) + (1,) * (len(shape) - dim - 1))

    factor_of = one(*split[0])
    for cut in split[1:]:
        factor_of = factor_of * one(*cut)
    return factor_of


def centred(own_key, extent, deviation, reach, shards=(), kind=jnp.bfloat16):
    loudness = block_levels(own_key, extent, shards, -0.22, 0.18) if shards else 1.0
    drawn = jax.random.normal(own_key, extent, jnp.float32) * deviation * loudness
    return jnp.minimum(jnp.maximum(drawn, -reach), reach).astype(kind)


def setup_inputs(seed: int = 0) -> dict:
    streams_of = jax.random.split(jax.random.key(seed), 9)
    inverse_pool = centred(streams_of[0], (NP, NP), 1.0, 6.0, ((0, 8), (1, 4)), jnp.float32)
    panel_one = centred(streams_of[1], (NP, W), (NSEL1 * BLK) ** -0.5, 0.1875, ((0, 32),), jnp.float32)
    panel_two = centred(streams_of[2], (NP, W), (NSEL2 * BLK) ** -0.5, 0.21875, ((0, 32),), jnp.float32)
    upper_two = centred(streams_of[3], (W, W), W ** -0.5, 0.25, (), jnp.float32)
    lower_one = draw_lower_one(jax.random.fold_in(streams_of[8], 71), 0)
    lower_two = draw_lower_two(jax.random.fold_in(streams_of[8], 71), 0)
    list_one = draw_list_one(jax.random.fold_in(streams_of[8], 71), 0)
    list_two = draw_list_two(jax.random.fold_in(streams_of[8], 71), 0)
    return dict(inverse_pool=inverse_pool, panel_one=panel_one, panel_two=panel_two, upper_two=upper_two, lower_one=lower_one, lower_two=lower_two, list_one=list_one, list_two=list_two)


def product(left, right):
    return jnp.dot(left, right, precision=lax.Precision.HIGHEST, preferred_element_type=jnp.float32)


def transposed_product(left, right):
    return lax.dot_general(left, right, (((0,), (0,)), ((), ())), precision=lax.Precision.HIGHEST, preferred_element_type=jnp.float32)


def live_rows(listing):
    blocks = jnp.arange(NP, dtype=jnp.int32) // BLK
    hits = jnp.any(blocks[:, None] == listing[None, :].astype(jnp.int32), axis=1)
    return jnp.where(hits, 1.0, 0.0).astype(jnp.float32)[:, None]


def reference(inverse_pool, panel_one, panel_two, upper_two, lower_one, lower_two, list_one, list_two):
    live_one = live_rows(list_one)
    live_two = live_rows(list_two)
    masked_one = live_one * panel_one
    masked_two = live_two * panel_two
    first_offdiag = -live_one * product(inverse_pool, masked_one)
    first_diag = transposed_product(lower_one, lower_one) - transposed_product(masked_one, first_offdiag)
    second_offdiag = -live_two * (product(first_offdiag, upper_two) + product(inverse_pool, masked_two))
    second_coupling = -(product(first_diag, upper_two) + transposed_product(first_offdiag, masked_two))
    second_diag = transposed_product(lower_two, lower_two) - transposed_product(upper_two, second_coupling) - transposed_product(masked_two, second_offdiag)
    return first_offdiag, first_diag, second_offdiag, second_coupling, second_diag
```

```python
import functools

import jax
import jax.numpy as jnp
from jax import lax
from jax.experimental import pallas as pl
from jax.experimental.pallas import tpu as pltpu
from jax.sharding import PartitionSpec as P

BLK = 128
MESH = pl.DeviceIdType.MESH


def halves(value):
    high = value.astype(jnp.bfloat16)
    low = (value - high.astype(jnp.float32)).astype(jnp.bfloat16)
    return high, low


def split_dot(left, right, dims):
    def one(a, b):
        return lax.dot_general(a, b, (dims, ((), ())), preferred_element_type=jnp.float32)

    return one(left[0], right[0]) + (one(left[0], right[1]) + one(left[1], right[0]))


PLAIN = ((1,), (0,))
FIRST = ((0,), (0,))


def live_column(listing, first_row, count):
    blocks = (first_row + lax.broadcasted_iota(jnp.int32, (count, 1), 0)) // BLK

    def step(k, hits):
        return jnp.maximum(hits, jnp.where(blocks == listing[k], 1.0, 0.0).astype(jnp.float32))

    return lax.fori_loop(0, listing.shape[0], step, jnp.zeros((count, 1), jnp.float32))


def body(
    R, C, nsend,
    x_in, one_in, two_in, u_in, l1_in, l2_in, list1, list2,
    f_out, d1_out, s_out, c_out, d2_out,
    x_v, u_v, l1_v, l2_v, zbuf, mcol, mrow, abuf, arecv, asum, frow, qbuf, qrecv, qfull, wt,
    load_sem, send_sem, z_sem, m_sem, g_sem, a_sem, f_sem, q_sem, gz_sem, gx_sem, gy_sem, gc_sem,
):
    g = R // C
    span, W = one_in.shape
    rows, K = x_in.shape
    wc = W // C
    ch = 3 * W // R
    p, c = lax.axis_index("prow"), lax.axis_index("pcol")
    z, i = p // g, p % g
    partner = c + 1 - 2 * (c % 2)
    panels = (one_in, two_in)
    pending = []

    def remote(src, dst, recv_sem, to):
        return pltpu.make_async_remote_copy(
            src_ref=src, dst_ref=dst, send_sem=send_sem.at[len(pending)],
            recv_sem=recv_sem, device_id=to, device_id_type=MESH,
        )

    def send(src, dst, recv_sem, to, when=None):
        copy = remote(src, dst, recv_sem, to)
        pending.append((copy, when))
        if when is None:
            copy.start()
        else:
            pl.when(when)(copy.start)

    def arrived(dst, recv_sem):
        pltpu.make_async_copy(dst, dst, recv_sem).wait()

    def at(base, index, size):
        return base.at[pl.ds(pl.multiple_of(index * size, 8), size)]

    loads = []
    for k, (src, dst) in enumerate(((x_in, x_v), (l1_in, l1_v), (l2_in, l2_v), (u_in, u_v))):
        copy = pltpu.make_async_copy(src, dst, load_sem.at[k])
        copy.start()
        loads.append(copy)

    barrier = pltpu.get_barrier_semaphore()
    peers = 0
    for dp in range(1, R):
        pl.semaphore_signal(barrier, inc=1, device_id=((p + dp) % R, c), device_id_type=MESH)
        peers += 1
    for di in range(g):
        for dc in range(1, C):
            pl.semaphore_signal(
                barrier, inc=1, device_id=(z * g + (i + di) % g, (c + dc) % C), device_id_type=MESH
            )
            peers += 1
    pl.semaphore_wait(barrier, peers)

    for k in range(2):
        for dz in range(1, C):
            send(panels[k], zbuf.at[k, dz], z_sem.at[k, dz], (((z + dz) % C) * g + i, c))

    own = i * C + c

    def to_columns(k, dz):
        plane = (z + C - dz) % C
        src = panels[k] if dz == 0 else zbuf.at[k, dz]
        dst, sem = at(mcol.at[k], own, span), m_sem.at[k, own]
        for di in range(g):
            to = (z * g + (i + di) % g, plane)
            if di:
                send(src, dst, sem, to)
            else:
                send(src, dst, sem, to, plane != c)
                pl.when(plane == c)(pltpu.make_async_copy(src, dst, sem).start)

    for k in range(2):
        to_columns(k, 0)
    for k in range(2):
        for dz in range(1, C):
            arrived(zbuf.at[k, dz], z_sem.at[k, dz])
            to_columns(k, dz)

    for k in range(2):
        dst, sem = at(mrow.at[k], c, span), g_sem.at[k, c]
        pltpu.make_async_copy(panels[k], dst, sem).start()
        for dc in range(2, C, 2):
            send(panels[k], dst, sem, (p, (c + dc) % C))
        send(panels[k], dst, sem, (p, partner))

    for copy in loads:
        copy.wait()
    for src, dst in ((l1_v, d1_out), (l2_v, d2_out)):
        pair = halves(src[...])
        dst[...] = split_dot(pair, pair, FIRST)

    for k in range(2):
        for dc in range(2, C, 2):
            other = (c + dc) % C
            piece = at(mrow.at[k], other, span)
            arrived(piece, g_sem.at[k, other])
            send(piece, piece, g_sem.at[k, other], (p, partner))

    x_pair = halves(x_v[...])
    for k, listing in enumerate((list1, list2)):
        for j in range(g * C):
            arrived(mcol.at[k, pl.ds(j * span, span)], m_sem.at[k, j])
        masked = live_column(listing, c * K, K) * mcol[k]
        product = split_dot(x_pair, halves(masked), PLAIN)
        for cc in range(C):
            abuf[k, cc] = product[:, cc * wc:(cc + 1) * wc]
        for dc in range(1, C):
            other = (c + dc) % C
            send(abuf.at[k, other], arecv.at[k, dc], a_sem.at[k, dc], (p, other))

    row_one, row_two = live_column(list1, p * rows, rows), live_column(list2, p * rows, rows)
    for k in range(2):
        arrived(at(mrow.at[k], c, span), g_sem.at[k, c])
        for dc in range(0, C, 2):
            other = (partner + dc) % C
            arrived(at(mrow.at[k], other, span), g_sem.at[k, other])
    left_one = halves(row_one * mrow[0])
    left_two = halves(row_two * mrow[1])

    def total(k, mask):
        result = abuf[k, c]
        for dc in range(1, C):
            arrived(arecv.at[k, dc], a_sem.at[k, dc])
            result = result + arecv[k, dc]
        result = mask * result
        asum[k] = result
        return halves(result)

    right = total(0, row_one)
    qbuf[0:W] = split_dot(left_one, right, FIRST)
    cross = split_dot(right, left_two, FIRST)
    for cc in range(C):
        qbuf[W + cc * wc:W + (cc + 1) * wc] = cross[:, cc * wc:(cc + 1) * wc]
    right = total(1, row_two)
    qbuf[2 * W:3 * W] = split_dot(left_two, right, FIRST)

    for dp in range(1, R):
        other = (p + dp) % R
        send(at(qbuf, other, ch), qrecv.at[dp], q_sem.at[dp], (other, c))
    for k in range(2):
        for dc in range(1, C):
            other = (c + dc) % C
            send(at(asum.at[k], other, span), frow.at[k, c], f_sem.at[k, c], (p, other))
        frow[k, c] = asum[k, pl.ds(pl.multiple_of(c * span, 8), span)]

    result = qbuf[pl.ds(pl.multiple_of(p * ch, 8), ch)]
    for dp in range(1, R):
        arrived(qrecv.at[dp], q_sem.at[dp])
        result = result + qrecv[dp]
    qfull[c, pl.ds(pl.multiple_of(p * ch, 8), ch)] = result

    def chunk(dz, di, dc, base):
        rank = ((z + C - dz) % C) * g + (i + g - di) % g
        return at(qfull.at[(base + C - dc) % C], rank, ch)

    def onward(dz, di):
        piece = chunk(dz, di, 0, c)
        for dc in range(2, C, 2):
            send(piece, piece, gy_sem.at[dz, di, dc // 2], (p, (c + dc) % C))
        send(piece, piece, gc_sem.at[dz, di, 0], (p, partner))

    piece = chunk(0, 0, 0, c)
    for dz in range(1, C):
        send(piece, piece, gz_sem.at[dz], (((z + dz) % C) * g + i, c))
    for dz in range(C):
        piece = chunk(dz, 0, 0, c)
        if dz:
            arrived(piece, gz_sem.at[dz])
        for di in range(1, g):
            send(piece, piece, gx_sem.at[dz, di], (z * g + (i + di) % g, c))
        onward(dz, 0)
    for dz in range(C):
        for di in range(1, g):
            arrived(chunk(dz, di, 0, c), gx_sem.at[dz, di])
            onward(dz, di)

    u_pair = halves(u_v[...])
    for k in range(2):
        for dc in range(1, C):
            other = (c + dc) % C
            arrived(frow.at[k, other], f_sem.at[k, other])
    first_row = p * rows + c * span
    for cc in range(C):
        f_out[:, cc * wc:(cc + 1) * wc] = -frow[0, cc]
        s_out[:, cc * wc:(cc + 1) * wc] = frow[1, cc]
    f_u = split_dot(halves(f_out[...]), u_pair, PLAIN)
    s_out[...] = -live_column(list2, first_row, span) * (f_u + s_out[...])

    for dz in range(C):
        for di in range(g):
            for dc in range(2, C, 2):
                piece = chunk(dz, di, dc, c)
                arrived(piece, gy_sem.at[dz, di, dc // 2])
                send(piece, piece, gc_sem.at[dz, di, dc // 2], (p, partner))
    for dz in range(C):
        for di in range(g):
            for dc in range(0, C, 2):
                arrived(chunk(dz, di, dc, partner), gc_sem.at[dz, di, dc // 2])

    for cc in range(C):
        lanes = slice(cc * wc, (cc + 1) * wc)
        d1_out[:, lanes] += qfull[cc, 0:W]
        for k in range(C):
            wt[lanes, k * wc:(k + 1) * wc] = qfull[cc, W + k * wc:W + (k + 1) * wc]
        d2_out[:, lanes] += qfull[cc, 2 * W:3 * W]
    c_out[...] = wt[...] - split_dot(halves(d1_out[...]), u_pair, PLAIN)
    d2_out[...] -= split_dot(u_pair, halves(c_out[...]), FIRST) + split_dot(
        halves(wt[...]), u_pair, FIRST
    )

    assert len(pending) == nsend
    for copy, when in pending:
        if when is None:
            copy.wait_send()
        else:
            pl.when(when)(copy.wait_send)


def solution(mesh):
    R, C = mesh.shape["prow"], mesh.shape["pcol"]
    g = R // C

    def local(inverse_pool, panel_one, panel_two, upper_two, lower_one, lower_two, list_one, list_two):
        span, W = panel_one.shape
        rows, K = inverse_pool.shape
        wc, ch = W // C, 3 * W // R
        half = C // 2
        nsend = (
            2 * (C - 1) + 2 * C * g + 2 * half + 2 * (half - 1) + 2 * (C - 1) + (R - 1) + 2 * (C - 1)
            + (C - 1) + C * (g - 1) + C * g * half + C * g * (half - 1)
        )
        f32, dma = jnp.float32, pltpu.SemaphoreType.DMA
        block = jax.ShapeDtypeStruct((W, W), f32)
        strip = jax.ShapeDtypeStruct((span, W), f32)
        return pl.pallas_call(
            functools.partial(body, R, C, nsend),
            out_shape=(strip, block, strip, block, block),
            in_specs=[pl.BlockSpec(memory_space=pl.ANY)] * 6
            + [pl.BlockSpec(memory_space=pltpu.SMEM)] * 2,
            out_specs=(pl.BlockSpec(memory_space=pltpu.VMEM),) * 5,
            scratch_shapes=[
                pltpu.VMEM((rows, K), f32),
                pltpu.VMEM((W, W), f32),
                pltpu.VMEM((W, W), f32),
                pltpu.VMEM((W, W), f32),
                pltpu.VMEM((2, C, span, W), f32),
                pltpu.VMEM((2, K, W), f32),
                pltpu.VMEM((2, rows, W), f32),
                pltpu.VMEM((2, C, rows, wc), f32),
                pltpu.VMEM((2, C, rows, wc), f32),
                pltpu.VMEM((2, rows, wc), f32),
                pltpu.VMEM((2, C, span, wc), f32),
                pltpu.VMEM((3 * W, wc), f32),
                pltpu.VMEM((R, ch, wc), f32),
                pltpu.VMEM((C, 3 * W, wc), f32),
                pltpu.VMEM((W, W), f32),
                dma((4,)),
                dma((nsend,)),
                dma((2, C)),
                dma((2, g * C)),
                dma((2, C)),
                dma((2, C)),
                dma((2, C)),
                dma((R,)),
                dma((C,)),
                dma((C, g)),
                dma((C, g, half)),
                dma((C, g, half)),
            ],
            compiler_params=pltpu.CompilerParams(collective_id=0, has_side_effects=True),
        )(inverse_pool, panel_one, panel_two, upper_two, lower_one, lower_two, list_one, list_two)

    return jax.shard_map(
        local,
        mesh=mesh,
        in_specs=(
            P("prow", "pcol"),
            P(("prow", "pcol"), None),
            P(("prow", "pcol"), None),
            P(),
            P(),
            P(),
            P(),
            P(),
        ),
        out_specs=(P(("prow", "pcol"), None), P(), P(("prow", "pcol"), None), P(), P()),
        check_vma=False,
    )
```

```python
import functools

import jax
import jax.numpy as jnp
from jax import lax
from jax.experimental import pallas as pl
from jax.experimental.pallas import tpu as pltpu
from jax.sharding import PartitionSpec as P

BLK = 128
MESH = pl.DeviceIdType.MESH


def halves(value):
    high = value.astype(jnp.bfloat16)
    low = (value - high.astype(jnp.float32)).astype(jnp.bfloat16)
    return high, low


def split_dot(left, right, dims):
    def one(a, b):
        return lax.dot_general(a, b, (dims, ((), ())), preferred_element_type=jnp.float32)

    return one(left[0], right[0]) + (one(left[0], right[1]) + one(left[1], right[0]))


PLAIN = ((1,), (0,))
FIRST = ((0,), (0,))


def live_column(listing, first_row, count):
    blocks = (first_row + lax.broadcasted_iota(jnp.int32, (count, 1), 0)) // BLK

    def step(k, hits):
        return jnp.maximum(hits, jnp.where(blocks == listing[k], 1.0, 0.0).astype(jnp.float32))

    return lax.fori_loop(0, listing.shape[0], step, jnp.zeros((count, 1), jnp.float32))


def body(
    R, C, nsend,
    x_in, one_in, two_in, u_in, l1_in, l2_in, list1, list2,
    f_out, d1_out, s_out, c_out, d2_out,
    x_v, u_v, l1_v, l2_v, zbuf, mcol, mrow, abuf, arecv, brecv, asum, frow, qbuf, xrecv, xsum, zrecv, qfull, wt,
    load_sem, send_sem, z_sem, m_sem, g_sem, a_sem, b_sem, f_sem, x_sem, q_sem, gz_sem, gx_sem, gy_sem, gc_sem,
):
    g, half = R // C, C // 2
    span, W = one_in.shape
    rows, K = x_in.shape
    wc = W // C
    part, ch = W // g, W // R
    p, c = lax.axis_index("prow"), lax.axis_index("pcol")
    z, i = p // g, p % g
    partner = c + 1 - 2 * (c % 2)
    panels = (one_in, two_in)
    pending = []

    def send(src, dst, recv_sem, to, when=None):
        copy = pltpu.make_async_remote_copy(
            src_ref=src, dst_ref=dst, send_sem=send_sem.at[len(pending)],
            recv_sem=recv_sem, device_id=to, device_id_type=MESH,
        )
        pending.append((copy, when))
        if when is None:
            copy.start()
        else:
            pl.when(when)(copy.start)

    def arrived(dst, recv_sem):
        pltpu.make_async_copy(dst, dst, recv_sem).wait()

    def at(base, index, size):
        return base.at[pl.ds(pl.multiple_of(index * size, 8), size)]

    def plane_peer(dz):
        return (((z + dz) % C) * g + i, c)

    def side_peer(di):
        return (z * g + (i + di) % g, c)

    loads = []
    for k, (src, dst) in enumerate(((l1_in, l1_v), (l2_in, l2_v), (x_in, x_v), (u_in, u_v))):
        copy = pltpu.make_async_copy(src, dst, load_sem.at[k])
        copy.start()
        loads.append(copy)

    barrier = pltpu.get_barrier_semaphore()
    peers = 0
    for dp in range(1, R):
        pl.semaphore_signal(barrier, inc=1, device_id=((p + dp) % R, c), device_id_type=MESH)
        peers += 1
    for di in range(g):
        for dc in range(1, C):
            pl.semaphore_signal(
                barrier, inc=1, device_id=(z * g + (i + di) % g, (c + dc) % C), device_id_type=MESH
            )
            peers += 1
    pl.semaphore_wait(barrier, peers)

    def to_columns(k, dz):
        plane = (z + C - dz) % C
        src = panels[k] if dz == 0 else zbuf.at[k, dz]
        own = i * C + c
        dst, sem = at(mcol.at[k], own, span), m_sem.at[k, own]
        send(src, dst, sem, (p, plane), plane != c)
        pl.when(plane == c)(pltpu.make_async_copy(src, dst, sem).start)
        for di in range(1, g):
            send(src, dst, sem, (z * g + (i + di) % g, plane), plane // 2 == c // 2)

    def far(dy, parity):
        return ((c // 2 + dy) % half) * 2 + parity

    def across(k):
        for dy in range(1, half):
            for parity in range(2):
                slot = i * C + far(dy, parity)
                piece = at(mcol.at[k], slot, span)
                arrived(piece, m_sem.at[k, slot])
                for di in range(1, g):
                    send(piece, piece, m_sem.at[k, slot], side_peer(di))

    def columns_arrived(k):
        for dy in range(half):
            for parity in range(2):
                for di in range(1 if dy else 0, g):
                    slot = ((i + di) % g) * C + far(dy, parity)
                    arrived(at(mcol.at[k], slot, span), m_sem.at[k, slot])

    def to_row(k):
        dst, sem = at(mrow.at[k], c, span), g_sem.at[k, c]
        pltpu.make_async_copy(panels[k], dst, sem).start()
        for dc in range(2, C, 2):
            send(panels[k], dst, sem, (p, (c + dc) % C))
        send(panels[k], dst, sem, (p, partner))

    def row_onward(k):
        for dc in range(2, C, 2):
            other = (c + dc) % C
            piece = at(mrow.at[k], other, span)
            arrived(piece, g_sem.at[k, other])
            send(piece, piece, g_sem.at[k, other], (p, partner))

    def row_arrived(k):
        arrived(at(mrow.at[k], c, span), g_sem.at[k, c])
        for dc in range(0, C, 2):
            other = (partner + dc) % C
            arrived(at(mrow.at[k], other, span), g_sem.at[k, other])

    def tile_product(k, listing):
        columns_arrived(k)
        masked = live_column(listing, c * K, K) * mcol[k]
        product = split_dot(x_pair, halves(masked), PLAIN)
        for cc in range(C):
            abuf[k, cc] = product[:, cc * wc:(cc + 1) * wc]
        for j in range(half):
            send(abuf.at[k, (partner + 2 * j) % C], arecv.at[k, j], a_sem.at[k, j], (p, partner))

    def pair_sum(k):
        for j in list(range(1, half)) + [0]:
            other = (c + 2 * j) % C
            arrived(arecv.at[k, j], a_sem.at[k, j])
            abuf[k, other] = abuf[k, other] + arecv[k, j]
            if j:
                send(abuf.at[k, other], brecv.at[k, j], b_sem.at[k, j], (p, other))

    def total(k, mask):
        result = abuf[k, c]
        for j in range(1, half):
            arrived(brecv.at[k, j], b_sem.at[k, j])
            result = result + brecv[k, j]
        result = mask * result
        asum[k] = result
        return halves(result)

    def rows_out(k):
        for dc in range(1, C):
            other = (c + dc) % C
            send(at(asum.at[k], other, span), frow.at[k, c], f_sem.at[k, c], (p, other))
        frow[k, c] = asum[k, pl.ds(pl.multiple_of(c * span, 8), span)]

    def side_out(b):
        for di in range(1, g):
            other = (i + di) % g
            send(at(qbuf.at[b], other, part), xrecv.at[b, di], x_sem.at[b, di], side_peer(di))

    def side_in(b):
        result = qbuf[b, pl.ds(pl.multiple_of(i * part, 8), part)]
        for di in range(1, g):
            arrived(xrecv.at[b, di], x_sem.at[b, di])
            result = result + xrecv[b, di]
        xsum[b] = result
        for dz in range(1, C):
            send(at(xsum.at[b], (z + dz) % C, ch), zrecv.at[b, dz], q_sem.at[b, dz], plane_peer(dz))

    def block(b, column, side, plane):
        first = b * W + side * part + plane * ch
        return qfull.at[column, pl.ds(pl.multiple_of(first, 8), ch)]

    def block_part(b, column, side):
        return qfull.at[column, pl.ds(pl.multiple_of(b * W + side * part, 8), part)]

    def plane_in(b):
        result = xsum[b, pl.ds(pl.multiple_of(z * ch, 8), ch)]
        for dz in range(1, C):
            arrived(zrecv.at[b, dz], q_sem.at[b, dz])
            result = result + zrecv[b, dz]
        piece = block(b, c, i, z)
        piece[...] = result
        for dz in range(1, C):
            send(piece, piece, gz_sem.at[b, dz], plane_peer(dz))

    def onward(b, di):
        piece = block_part(b, c, (i + g - di) % g)
        for dc in range(2, C, 2):
            send(piece, piece, gy_sem.at[b, di, dc // 2], (p, (c + dc) % C))
        send(piece, piece, gc_sem.at[b, di, 0], (p, partner))

    def gather_side(b):
        for dz in range(1, C):
            arrived(block(b, c, i, (z + C - dz) % C), gz_sem.at[b, dz])
        piece = block_part(b, c, i)
        for di in range(1, g):
            send(piece, piece, gx_sem.at[b, di], side_peer(di))
        onward(b, 0)

    def gather_row(b):
        for di in range(1, g):
            arrived(block_part(b, c, (i + g - di) % g), gx_sem.at[b, di])
            onward(b, di)

    def gather_core(b):
        for di in range(g):
            for dc in range(2, C, 2):
                piece = block_part(b, (c + C - dc) % C, (i + g - di) % g)
                arrived(piece, gy_sem.at[b, di, dc // 2])
                send(piece, piece, gc_sem.at[b, di, dc // 2], (p, partner))

    def gathered(b):
        for di in range(g):
            for dc in range(0, C, 2):
                piece = block_part(b, (partner + C - dc) % C, (i + g - di) % g)
                arrived(piece, gc_sem.at[b, di, dc // 2])

    for k in range(2):
        for dz in range(1, C):
            send(panels[k], zbuf.at[k, dz], z_sem.at[k, dz], plane_peer(dz))
        to_columns(k, 0)
    for copy in loads[:2]:
        copy.wait()
    for src, dst in ((l1_v, d1_out), (l2_v, d2_out)):
        pair = halves(src[...])
        dst[...] = split_dot(pair, pair, FIRST)
    for k in range(2):
        for dz in range(1, C):
            arrived(zbuf.at[k, dz], z_sem.at[k, dz])
            to_columns(k, dz)
        to_row(k)
        if k == 0:
            across(0)
            for copy in loads[2:]:
                copy.wait()
            x_pair = halves(x_v[...])
            row_one, row_two = live_column(list1, p * rows, rows), live_column(list2, p * rows, rows)
    row_onward(0)
    tile_product(0, list1)
    across(1)
    pair_sum(0)
    row_onward(1)
    row_arrived(0)
    left = halves(row_one * mrow[0])
    right_one = total(0, row_one)
    qbuf[0] = split_dot(left, right_one, FIRST)
    side_out(0)
    tile_product(1, list2)
    pair_sum(1)
    row_arrived(1)
    left = halves(row_two * mrow[1])
    cross = split_dot(right_one, left, FIRST)
    for cc in range(C):
        qbuf[1, cc * wc:(cc + 1) * wc] = cross[:, cc * wc:(cc + 1) * wc]
    side_out(1)
    side_in(0)
    right_two = total(1, row_two)
    qbuf[2] = split_dot(left, right_two, FIRST)
    side_out(2)
    plane_in(0)
    side_in(1)
    gather_side(0)
    plane_in(1)
    side_in(2)
    gather_row(0)
    gather_side(1)
    plane_in(2)
    gather_core(0)
    gather_row(1)
    gather_side(2)
    rows_out(0)
    rows_out(1)
    gather_core(1)
    gather_row(2)

    u_pair = halves(u_v[...])
    gathered(0)
    for cc in range(C):
        d1_out[:, cc * wc:(cc + 1) * wc] += qfull[cc, 0:W]
    d1_u = split_dot(halves(d1_out[...]), u_pair, PLAIN)
    gather_core(2)
    for k in range(2):
        for dc in range(1, C):
            other = (c + dc) % C
            arrived(frow.at[k, other], f_sem.at[k, other])
    for cc in range(C):
        f_out[:, cc * wc:(cc + 1) * wc] = -frow[0, cc]
        s_out[:, cc * wc:(cc + 1) * wc] = frow[1, cc]
    f_u = split_dot(halves(f_out[...]), u_pair, PLAIN)
    s_out[...] = -live_column(list2, p * rows + c * span, span) * (f_u + s_out[...])

    gathered(1)
    for cc in range(C):
        for k in range(C):
            wt[cc * wc:(cc + 1) * wc, k * wc:(k + 1) * wc] = qfull[cc, W + k * wc:W + (k + 1) * wc]
    c_out[...] = wt[...] - d1_u
    d2_out[...] -= split_dot(u_pair, halves(c_out[...]), FIRST) + split_dot(
        halves(wt[...]), u_pair, FIRST
    )
    gathered(2)
    for cc in range(C):
        d2_out[:, cc * wc:(cc + 1) * wc] += qfull[cc, 2 * W:3 * W]

    assert len(pending) == nsend, len(pending)
    for copy, when in pending:
        if when is None:
            copy.wait_send()
        else:
            pl.when(when)(copy.wait_send)


def solution(mesh):
    R, C = mesh.shape["prow"], mesh.shape["pcol"]
    g = R // C

    def local(inverse_pool, panel_one, panel_two, upper_two, lower_one, lower_two, list_one, list_two):
        span, W = panel_one.shape
        rows, K = inverse_pool.shape
        wc, half = W // C, C // 2
        panel = (C - 1) + C * g + 2 * (half - 1) * (g - 1) + half + (half - 1)
        reduced = half + (half - 1) + (C - 1)
        gram = (g - 1) + 2 * (C - 1) + (g - 1) + g * half + g * (half - 1)
        nsend = 2 * panel + 2 * reduced + 3 * gram
        f32, dma = jnp.float32, pltpu.SemaphoreType.DMA
        block = jax.ShapeDtypeStruct((W, W), f32)
        strip = jax.ShapeDtypeStruct((span, W), f32)
        return pl.pallas_call(
            functools.partial(body, R, C, nsend),
            out_shape=(strip, block, strip, block, block),
            in_specs=[pl.BlockSpec(memory_space=pl.ANY)] * 6
            + [pl.BlockSpec(memory_space=pltpu.SMEM)] * 2,
            out_specs=(pl.BlockSpec(memory_space=pltpu.VMEM),) * 5,
            scratch_shapes=[
                pltpu.VMEM((rows, K), f32),
                pltpu.VMEM((W, W), f32),
                pltpu.VMEM((W, W), f32),
                pltpu.VMEM((W, W), f32),
                pltpu.VMEM((2, C, span, W), f32),
                pltpu.VMEM((2, K, W), f32),
                pltpu.VMEM((2, rows, W), f32),
                pltpu.VMEM((2, C, rows, wc), f32),
                pltpu.VMEM((2, half, rows, wc), f32),
                pltpu.VMEM((2, half, rows, wc), f32),
                pltpu.VMEM((2, rows, wc), f32),
                pltpu.VMEM((2, C, span, wc), f32),
                pltpu.VMEM((3, W, wc), f32),
                pltpu.VMEM((3, g, W // g, wc), f32),
                pltpu.VMEM((3, W // g, wc), f32),
                pltpu.VMEM((3, C, W // R, wc), f32),
                pltpu.VMEM((C, 3 * W, wc), f32),
                pltpu.VMEM((W, W), f32),
                dma((4,)),
                dma((nsend,)),
                dma((2, C)),
                dma((2, g * C)),
                dma((2, C)),
                dma((2, half)),
                dma((2, half)),
                dma((2, C)),
                dma((3, g)),
                dma((3, C)),
                dma((3, C)),
                dma((3, g)),
                dma((3, g, half)),
                dma((3, g, half)),
            ],
            compiler_params=pltpu.CompilerParams(collective_id=0, has_side_effects=True),
        )(inverse_pool, panel_one, panel_two, upper_two, lower_one, lower_two, list_one, list_two)

    return jax.shard_map(
        local,
        mesh=mesh,
        in_specs=(
            P("prow", "pcol"),
            P(("prow", "pcol"), None),
            P(("prow", "pcol"), None),
            P(),
            P(),
            P(),
            P(),
            P(),
        ),
        out_specs=(P(("prow", "pcol"), None), P(), P(("prow", "pcol"), None), P(), P()),
        check_vma=False,
    )
```

```python
import functools

import jax
import jax.numpy as jnp
from jax import lax
from jax.experimental import pallas as pl
from jax.experimental.pallas import tpu as pltpu
from jax.sharding import PartitionSpec as P

BLK = 128
MESH = pl.DeviceIdType.MESH


def halves(value):
    high = value.astype(jnp.bfloat16)
    low = (value - high.astype(jnp.float32)).astype(jnp.bfloat16)
    return high, low


def split_dot(left, right, dims):
    def one(a, b):
        return lax.dot_general(a, b, (dims, ((), ())), preferred_element_type=jnp.float32)

    return one(left[0], right[0]) + (one(left[0], right[1]) + one(left[1], right[0]))


PLAIN = ((1,), (0,))
FIRST = ((0,), (0,))


def live_column(listing, first_row, count):
    blocks = (first_row + lax.broadcasted_iota(jnp.int32, (count, 1), 0)) // BLK

    def step(k, hits):
        return jnp.maximum(hits, jnp.where(blocks == listing[k], 1.0, 0.0).astype(jnp.float32))

    return lax.fori_loop(0, listing.shape[0], step, jnp.zeros((count, 1), jnp.float32))


def write_out(*refs):
    sems = refs[-1]
    copies = [pltpu.make_async_copy(refs[k], refs[5 + k], sems.at[k]) for k in range(5)]
    for copy in copies:
        copy.start()
    for copy in copies:
        copy.wait()


def body(
    R, C, nsend,
    x_in, one_in, two_in, u_in, l1_in, l2_in, list1, list2,
    f_out, d1_out, s_out, c_out, d2_out,
    x_v, u_v, l1_v, l2_v, zbuf, mcol, mrow, abuf, arecv, brecv, asum, frow, qbuf, xrecv, xsum, zrecv, qfull, wt,
    load_sem, send_sem, z_sem, m_sem, g_sem, a_sem, b_sem, f_sem, x_sem, q_sem, gz_sem, gx_sem, gy_sem, gc_sem,
):
    g, half = R // C, C // 2
    span, W = one_in.shape
    rows, K = x_in.shape
    wc = W // C
    part, ch = W // g, W // R
    p, c = lax.axis_index("prow"), lax.axis_index("pcol")
    z, i = p // g, p % g
    partner = c + 1 - 2 * (c % 2)
    panels = (one_in, two_in)
    pending = []

    def send(src, dst, recv_sem, to, when=None):
        copy = pltpu.make_async_remote_copy(
            src_ref=src, dst_ref=dst, send_sem=send_sem.at[len(pending)],
            recv_sem=recv_sem, device_id=to, device_id_type=MESH,
        )
        pending.append((copy, when))
        if when is None:
            copy.start()
        else:
            pl.when(when)(copy.start)

    def arrived(dst, recv_sem):
        pltpu.make_async_copy(dst, dst, recv_sem).wait()

    def at(base, index, size):
        return base.at[pl.ds(pl.multiple_of(index * size, 8), size)]

    def plane_peer(dz):
        return (((z + dz) % C) * g + i, c)

    def side_peer(di):
        return (z * g + (i + di) % g, c)

    loads = []
    for k, (src, dst) in enumerate(((l1_in, l1_v), (l2_in, l2_v), (x_in, x_v), (u_in, u_v))):
        copy = pltpu.make_async_copy(src, dst, load_sem.at[k])
        copy.start()
        loads.append(copy)

    barrier = pltpu.get_barrier_semaphore()
    peers = 0
    for dp in range(1, R):
        pl.semaphore_signal(barrier, inc=1, device_id=((p + dp) % R, c), device_id_type=MESH)
        peers += 1
    for di in range(g):
        for dc in range(1, C):
            pl.semaphore_signal(
                barrier, inc=1, device_id=(z * g + (i + di) % g, (c + dc) % C), device_id_type=MESH
            )
            peers += 1
    pl.semaphore_wait(barrier, peers)

    def to_columns(k, src, plane, valid=True):
        own = i * C + c
        dst, sem = at(mcol.at[k], own, span), m_sem.at[k, own]
        send(src, dst, sem, (p, plane), (plane != c) & valid)
        pl.when((plane == c) & valid)(pltpu.make_async_copy(src, dst, sem).start)
        for di in range(1, g):
            to = (z * g + (i + di) % g, plane)
            send(src, dst, sem, to, (plane // 2 == c // 2) & valid)

    def along(k, src, plane, way, valid=True):
        inside = (z + 1 < C) if way > 0 else (z > 0)
        send(src, zbuf.at[k, plane], z_sem.at[k, plane], plane_peer(way % C), inside & valid)

    def far(dy, parity):
        return ((c // 2 + dy) % half) * 2 + parity

    def across(k):
        for dy in range(1, half):
            for parity in range(2):
                slot = i * C + far(dy, parity)
                piece = at(mcol.at[k], slot, span)
                arrived(piece, m_sem.at[k, slot])
                for di in range(1, g):
                    send(piece, piece, m_sem.at[k, slot], side_peer(di))

    def columns_arrived(k):
        for dy in range(half):
            for parity in range(2):
                for di in range(1 if dy else 0, g):
                    slot = ((i + di) % g) * C + far(dy, parity)
                    arrived(at(mcol.at[k], slot, span), m_sem.at[k, slot])

    def to_row(k):
        dst, sem = at(mrow.at[k], c, span), g_sem.at[k, c]
        pltpu.make_async_copy(panels[k], dst, sem).start()
        for dc in range(2, C, 2):
            send(panels[k], dst, sem, (p, (c + dc) % C))
        send(panels[k], dst, sem, (p, partner))

    def row_onward(k):
        for dc in range(2, C, 2):
            other = (c + dc) % C
            piece = at(mrow.at[k], other, span)
            arrived(piece, g_sem.at[k, other])
            send(piece, piece, g_sem.at[k, other], (p, partner))

    def row_arrived(k):
        arrived(at(mrow.at[k], c, span), g_sem.at[k, c])
        for dc in range(0, C, 2):
            other = (partner + dc) % C
            arrived(at(mrow.at[k], other, span), g_sem.at[k, other])

    def tile_product(k, listing):
        columns_arrived(k)
        masked = live_column(listing, c * K, K) * mcol[k]
        product = split_dot(x_pair, halves(masked), PLAIN)
        for cc in range(C):
            abuf[k, cc] = product[:, cc * wc:(cc + 1) * wc]
        for j in range(half):
            send(abuf.at[k, (partner + 2 * j) % C], arecv.at[k, j], a_sem.at[k, j], (p, partner))

    def pair_sum(k):
        for j in list(range(1, half)) + [0]:
            other = (c + 2 * j) % C
            arrived(arecv.at[k, j], a_sem.at[k, j])
            abuf[k, other] = abuf[k, other] + arecv[k, j]
            if j:
                send(abuf.at[k, other], brecv.at[k, j], b_sem.at[k, j], (p, other))

    def total(k, mask):
        result = abuf[k, c]
        for j in range(1, half):
            arrived(brecv.at[k, j], b_sem.at[k, j])
            result = result + brecv[k, j]
        result = mask * result
        asum[k] = result
        return halves(result)

    def rows_out(k):
        for dc in range(1, C):
            other = (c + dc) % C
            send(at(asum.at[k], other, span), frow.at[k, c], f_sem.at[k, c], (p, other))
        frow[k, c] = asum[k, pl.ds(pl.multiple_of(c * span, 8), span)]

    def side_out(b):
        for di in range(1, g):
            other = (i + di) % g
            send(at(qbuf.at[b], other, part), xrecv.at[b, di], x_sem.at[b, di], side_peer(di))

    def side_in(b):
        result = qbuf[b, pl.ds(pl.multiple_of(i * part, 8), part)]
        for di in range(1, g):
            arrived(xrecv.at[b, di], x_sem.at[b, di])
            result = result + xrecv[b, di]
        xsum[b] = result
        for dz in range(1, C):
            send(at(xsum.at[b], (z + dz) % C, ch), zrecv.at[b, dz], q_sem.at[b, dz], plane_peer(dz))

    def block(b, column, side, plane):
        first = b * W + side * part + plane * ch
        return qfull.at[column, pl.ds(pl.multiple_of(first, 8), ch)]

    def block_part(b, column, side):
        return qfull.at[column, pl.ds(pl.multiple_of(b * W + side * part, 8), part)]

    def plane_in(b):
        result = xsum[b, pl.ds(pl.multiple_of(z * ch, 8), ch)]
        for dz in range(1, C):
            arrived(zrecv.at[b, dz], q_sem.at[b, dz])
            result = result + zrecv[b, dz]
        piece = block(b, c, i, z)
        piece[...] = result
        for dz in range(1, C):
            send(piece, piece, gz_sem.at[b, dz], plane_peer(dz))

    def gram_part(b, di, dc, base):
        return block_part(b, (base + C - dc) % C, (i + g - di) % g)

    def to_side(b, dc):
        piece = gram_part(b, 0, dc, c)
        for di in range(1, g):
            send(piece, piece, gx_sem.at[b, di, dc // 2], side_peer(di))

    def to_rows(b, di):
        piece = gram_part(b, di, 0, c)
        for dc in range(2, C, 2):
            send(piece, piece, gy_sem.at[b, di, dc // 2], (p, (c + dc) % C))

    def to_partner(b, di, dc):
        piece = gram_part(b, di, dc, c)
        send(piece, piece, gc_sem.at[b, di, dc // 2], (p, partner))

    def side_arrived(b, di, dc):
        arrived(gram_part(b, di, dc, c), gx_sem.at[b, di, dc // 2])

    def rows_arrived(b, di, dc):
        arrived(gram_part(b, di, dc, c), gy_sem.at[b, di, dc // 2])

    def gather_side(b):
        for dz in range(1, C):
            arrived(block(b, c, i, (z + C - dz) % C), gz_sem.at[b, dz])
        to_side(b, 0)
        to_rows(b, 0)
        to_partner(b, 0, 0)

    def gather_row(b):
        if b == 1:
            for dc in range(2, C, 2):
                rows_arrived(b, 0, dc)
                to_side(b, dc)
                to_partner(b, 0, dc)
        else:
            for di in range(1, g):
                side_arrived(b, di, 0)
                to_rows(b, di)
                to_partner(b, di, 0)

    def gather_core(b):
        if b == 1:
            for di in range(1, g):
                for dc in range(0, C, 2):
                    side_arrived(b, di, dc)
                    to_partner(b, di, dc)
        else:
            for di in range(g):
                for dc in range(2, C, 2):
                    rows_arrived(b, di, dc)
                    to_partner(b, di, dc)

    def gathered(b):
        for di in range(g):
            for dc in range(0, C, 2):
                piece = block_part(b, (partner + C - dc) % C, (i + g - di) % g)
                arrived(piece, gc_sem.at[b, di, dc // 2])

    for k in range(2):
        along(k, panels[k], z, 1)
        along(k, panels[k], z, -1)
        to_columns(k, panels[k], z)
    for copy in loads[:2]:
        copy.wait()
    for src, dst in ((l1_v, d1_out), (l2_v, d2_out)):
        pair = halves(src[...])
        dst[...] = split_dot(pair, pair, FIRST)
    for k in range(2):
        for dz in range(1, C):
            for way in (1, -1):
                valid = (z >= dz) if way > 0 else (z + dz < C)
                plane = (z + C - way * dz) % C
                src, sem = zbuf.at[k, plane], z_sem.at[k, plane]
                pl.when(valid)(functools.partial(arrived, src, sem))
                if dz < C - 1:
                    along(k, src, plane, way, valid)
                to_columns(k, src, plane, valid)
        to_row(k)
        if k == 0:
            across(0)
            for copy in loads[2:]:
                copy.wait()
            x_pair = halves(x_v[...])
            row_one, row_two = live_column(list1, p * rows, rows), live_column(list2, p * rows, rows)
    row_onward(0)
    tile_product(0, list1)
    across(1)
    pair_sum(0)
    row_onward(1)
    row_arrived(0)
    left = halves(row_one * mrow[0])
    right_one = total(0, row_one)
    qbuf[0] = split_dot(left, right_one, FIRST)
    side_out(0)
    tile_product(1, list2)
    pair_sum(1)
    row_arrived(1)
    left = halves(row_two * mrow[1])
    cross = split_dot(right_one, left, FIRST)
    for cc in range(C):
        qbuf[1, cc * wc:(cc + 1) * wc] = cross[:, cc * wc:(cc + 1) * wc]
    side_out(1)
    side_in(0)
    right_two = total(1, row_two)
    qbuf[2] = split_dot(left, right_two, FIRST)
    side_out(2)
    plane_in(0)
    side_in(1)
    gather_side(0)
    plane_in(1)
    side_in(2)
    gather_row(0)
    gather_side(1)
    plane_in(2)
    gather_core(0)
    gather_row(1)
    gather_side(2)
    rows_out(0)
    rows_out(1)
    gather_core(1)
    gather_row(2)

    u_pair = halves(u_v[...])
    gathered(0)
    for cc in range(C):
        d1_out[:, cc * wc:(cc + 1) * wc] += qfull[cc, 0:W]
    d1_u = split_dot(halves(d1_out[...]), u_pair, PLAIN)
    gather_core(2)
    for k in range(2):
        for dc in range(1, C):
            other = (c + dc) % C
            arrived(frow.at[k, other], f_sem.at[k, other])
    for cc in range(C):
        f_out[:, cc * wc:(cc + 1) * wc] = -frow[0, cc]
        s_out[:, cc * wc:(cc + 1) * wc] = frow[1, cc]
    f_u = split_dot(halves(f_out[...]), u_pair, PLAIN)
    s_out[...] = -live_column(list2, p * rows + c * span, span) * (f_u + s_out[...])

    gathered(1)
    for cc in range(C):
        for k in range(C):
            wt[cc * wc:(cc + 1) * wc, k * wc:(k + 1) * wc] = qfull[cc, W + k * wc:W + (k + 1) * wc]
    c_out[...] = wt[...] - d1_u
    d2_out[...] -= split_dot(u_pair, halves(c_out[...]), FIRST) + split_dot(
        halves(wt[...]), u_pair, FIRST
    )
    gathered(2)
    for cc in range(C):
        d2_out[:, cc * wc:(cc + 1) * wc] += qfull[cc, 2 * W:3 * W]

    assert len(pending) <= nsend
    for copy, when in pending:
        if when is None:
            copy.wait_send()
        else:
            pl.when(when)(copy.wait_send)


def solution(mesh):
    R, C = mesh.shape["prow"], mesh.shape["pcol"]
    g = R // C

    def local(inverse_pool, panel_one, panel_two, upper_two, lower_one, lower_two, list_one, list_two):
        span, W = panel_one.shape
        rows, K = inverse_pool.shape
        wc, half = W // C, C // 2
        panel = 2 * (C - 1) + (2 * C - 1) * g + 2 * (half - 1) * (g - 1) + half + (half - 1)
        reduced = half + (half - 1) + (C - 1)
        gram = (g - 1) + 2 * (C - 1) + (g - 1) + g * half + g * (half - 1)
        nsend = 2 * panel + 2 * reduced + 3 * gram
        f32, dma = jnp.float32, pltpu.SemaphoreType.DMA
        shapes = ((span, W), (W, W), (span, W), (W, W), (W, W))
        results = pl.pallas_call(
            functools.partial(body, R, C, nsend),
            out_shape=tuple(pltpu.VMEM(shape, f32) for shape in shapes),
            in_specs=[pl.BlockSpec(memory_space=pl.ANY)] * 6
            + [pl.BlockSpec(memory_space=pltpu.SMEM)] * 2,
            out_specs=(pl.BlockSpec(memory_space=pltpu.VMEM),) * 5,
            scratch_shapes=[
                pltpu.VMEM((rows, K), f32),
                pltpu.VMEM((W, W), f32),
                pltpu.VMEM((W, W), f32),
                pltpu.VMEM((W, W), f32),
                pltpu.VMEM((2, C, span, W), f32),
                pltpu.VMEM((2, K, W), f32),
                pltpu.VMEM((2, rows, W), f32),
                pltpu.VMEM((2, C, rows, wc), f32),
                pltpu.VMEM((2, half, rows, wc), f32),
                pltpu.VMEM((2, half, rows, wc), f32),
                pltpu.VMEM((2, rows, wc), f32),
                pltpu.VMEM((2, C, span, wc), f32),
                pltpu.VMEM((3, W, wc), f32),
                pltpu.VMEM((3, g, W // g, wc), f32),
                pltpu.VMEM((3, W // g, wc), f32),
                pltpu.VMEM((3, C, W // R, wc), f32),
                pltpu.VMEM((C, 3 * W, wc), f32),
                pltpu.VMEM((W, W), f32),
                dma((4,)),
                dma((nsend,)),
                dma((2, C)),
                dma((2, g * C)),
                dma((2, C)),
                dma((2, half)),
                dma((2, half)),
                dma((2, C)),
                dma((3, g)),
                dma((3, C)),
                dma((3, C)),
                dma((3, g, half)),
                dma((3, g, half)),
                dma((3, g, half)),
            ],
            compiler_params=pltpu.CompilerParams(collective_id=0, has_side_effects=True),
        )(inverse_pool, panel_one, panel_two, upper_two, lower_one, lower_two, list_one, list_two)
        return pl.pallas_call(
            write_out,
            out_shape=tuple(jax.ShapeDtypeStruct(shape, f32) for shape in shapes),
            in_specs=[pl.BlockSpec(memory_space=pl.ANY)] * 5,
            out_specs=(pl.BlockSpec(memory_space=pl.ANY),) * 5,
            scratch_shapes=[dma((5,))],
            compiler_params=pltpu.CompilerParams(vmem_limit_bytes=8 * W * W * 4),
        )(*results)

    return jax.shard_map(
        local,
        mesh=mesh,
        in_specs=(
            P("prow", "pcol"),
            P(("prow", "pcol"), None),
            P(("prow", "pcol"), None),
            P(),
            P(),
            P(),
            P(),
            P(),
        ),
        out_specs=(P(("prow", "pcol"), None), P(), P(("prow", "pcol"), None), P(), P()),
        check_vma=False,
    )
```

```python
import functools

import jax
import jax.numpy as jnp
from jax import lax
from jax.experimental import pallas as pl
from jax.experimental.pallas import tpu as pltpu
from jax.sharding import PartitionSpec as P

BLK = 128
MESH = pl.DeviceIdType.MESH


def halves(value):
    high = value.astype(jnp.bfloat16)
    low = (value - high.astype(jnp.float32)).astype(jnp.bfloat16)
    return high, low


def split_dot(left, right, dims):
    def one(a, b):
        return lax.dot_general(a, b, (dims, ((), ())), preferred_element_type=jnp.float32)

    return one(left[0], right[0]) + (one(left[0], right[1]) + one(left[1], right[0]))


PLAIN = ((1,), (0,))
FIRST = ((0,), (0,))


def live_column(listing, first_row, count):
    blocks = (first_row + lax.broadcasted_iota(jnp.int32, (count, 1), 0)) // BLK

    def step(k, hits):
        return jnp.maximum(hits, jnp.where(blocks == listing[k], 1.0, 0.0).astype(jnp.float32))

    return lax.fori_loop(0, listing.shape[0], step, jnp.zeros((count, 1), jnp.float32))


def write_out(*refs):
    sems = refs[-1]
    copies = [pltpu.make_async_copy(refs[k], refs[5 + k], sems.at[k]) for k in range(5)]
    for copy in copies:
        copy.start()
    for copy in copies:
        copy.wait()


def body(
    R, C, nsend,
    x_in, one_in, two_in, u_in, l1_in, l2_in, list1, list2,
    f_out, d1_out, s_out, c_out, d2_out,
    x_v, u_v, l1_v, l2_v, zbuf, mcol, mrow, abuf, arecv, brecv, asum, frow, qbuf, xrecv, xsum, zrecv, qfull, wt,
    load_sem, send_sem, z_sem, m_sem, g_sem, a_sem, b_sem, f_sem, x_sem, q_sem, gz_sem, gx_sem, gy_sem, gc_sem,
):
    g, half = R // C, C // 2
    span, W = one_in.shape
    rows, K = x_in.shape
    wc = W // C
    part, ch = W // g, W // R
    p, c = lax.axis_index("prow"), lax.axis_index("pcol")
    z, i = p // g, p % g
    partner = c + 1 - 2 * (c % 2)
    panels = (one_in, two_in)
    pending = []

    def send(src, dst, recv_sem, to, when=None):
        copy = pltpu.make_async_remote_copy(
            src_ref=src, dst_ref=dst, send_sem=send_sem.at[len(pending)],
            recv_sem=recv_sem, device_id=to, device_id_type=MESH,
        )
        pending.append((copy, when))
        if when is None:
            copy.start()
        else:
            pl.when(when)(copy.start)

    def arrived(dst, recv_sem):
        pltpu.make_async_copy(dst, dst, recv_sem).wait()

    def at(base, index, size):
        return base.at[pl.ds(pl.multiple_of(index * size, 8), size)]

    def plane_peer(dz):
        return (((z + dz) % C) * g + i, c)

    def side_peer(di):
        return (z * g + (i + di) % g, c)

    loads = []
    for k, (src, dst) in enumerate(((l1_in, l1_v), (l2_in, l2_v), (x_in, x_v), (u_in, u_v))):
        copy = pltpu.make_async_copy(src, dst, load_sem.at[k])
        copy.start()
        loads.append(copy)

    barrier = pltpu.get_barrier_semaphore()
    peers = 0
    for dp in range(1, R):
        pl.semaphore_signal(barrier, inc=1, device_id=((p + dp) % R, c), device_id_type=MESH)
        peers += 1
    for di in range(g):
        for dc in range(1, C):
            pl.semaphore_signal(
                barrier, inc=1, device_id=(z * g + (i + di) % g, (c + dc) % C), device_id_type=MESH
            )
            peers += 1
    pl.semaphore_wait(barrier, peers)

    def to_columns(k, src, plane, valid=True):
        own = i * C + c
        dst, sem = at(mcol.at[k], own, span), m_sem.at[k, own]
        send(src, dst, sem, (p, plane), (plane != c) & valid)
        pl.when((plane == c) & valid)(pltpu.make_async_copy(src, dst, sem).start)
        for di in range(1, g):
            to = (z * g + (i + di) % g, plane)
            send(src, dst, sem, to, (plane // 2 == c // 2) & valid)

    def along(k, src, plane, way, valid=True):
        inside = (z + 1 < C) if way > 0 else (z > 0)
        send(src, zbuf.at[k, plane], z_sem.at[k, plane], plane_peer(way % C), inside & valid)

    def far(dy, parity):
        return ((c // 2 + dy) % half) * 2 + parity

    def across(k):
        for dy in range(1, half):
            for parity in range(2):
                slot = i * C + far(dy, parity)
                piece = at(mcol.at[k], slot, span)
                arrived(piece, m_sem.at[k, slot])
                for di in range(1, g):
                    send(piece, piece, m_sem.at[k, slot], side_peer(di))

    def columns_arrived(k):
        for dy in range(half):
            for parity in range(2):
                for di in range(1 if dy else 0, g):
                    slot = ((i + di) % g) * C + far(dy, parity)
                    arrived(at(mcol.at[k], slot, span), m_sem.at[k, slot])

    def to_row(k):
        dst, sem = at(mrow.at[k], c, span), g_sem.at[k, c]
        pltpu.make_async_copy(panels[k], dst, sem).start()
        for dc in range(2, C, 2):
            send(panels[k], dst, sem, (p, (c + dc) % C))
        send(panels[k], dst, sem, (p, partner))

    def row_onward(k):
        for dc in range(2, C, 2):
            other = (c + dc) % C
            piece = at(mrow.at[k], other, span)
            arrived(piece, g_sem.at[k, other])
            send(piece, piece, g_sem.at[k, other], (p, partner))

    def row_arrived(k):
        arrived(at(mrow.at[k], c, span), g_sem.at[k, c])
        for dc in range(0, C, 2):
            other = (partner + dc) % C
            arrived(at(mrow.at[k], other, span), g_sem.at[k, other])

    def tile_product(k, listing):
        columns_arrived(k)
        masked = live_column(listing, c * K, K) * mcol[k]
        product = split_dot(x_pair, halves(masked), PLAIN)
        for cc in range(C):
            abuf[k, cc] = product[:, cc * wc:(cc + 1) * wc]
        for j in range(half):
            send(abuf.at[k, (partner + 2 * j) % C], arecv.at[k, j], a_sem.at[k, j], (p, partner))

    def pair_sum(k):
        for j in list(range(1, half)) + [0]:
            other = (c + 2 * j) % C
            arrived(arecv.at[k, j], a_sem.at[k, j])
            abuf[k, other] = abuf[k, other] + arecv[k, j]
            if j:
                send(abuf.at[k, other], brecv.at[k, j], b_sem.at[k, j], (p, other))

    def total(k, mask):
        result = abuf[k, c]
        for j in range(1, half):
            arrived(brecv.at[k, j], b_sem.at[k, j])
            result = result + brecv[k, j]
        result = mask * result
        asum[k] = result
        return halves(result)

    def rows_out(k):
        for dc in range(1, C):
            other = (c + dc) % C
            send(at(asum.at[k], other, span), frow.at[k, c], f_sem.at[k, c], (p, other))
        frow[k, c] = asum[k, pl.ds(pl.multiple_of(c * span, 8), span)]

    def side_out(b):
        for di in range(1, g):
            other = (i + di) % g
            send(at(qbuf.at[b], other, part), xrecv.at[b, di], x_sem.at[b, di], side_peer(di))

    def side_in(b):
        result = qbuf[b, pl.ds(pl.multiple_of(i * part, 8), part)]
        for di in range(1, g):
            arrived(xrecv.at[b, di], x_sem.at[b, di])
            result = result + xrecv[b, di]
        xsum[b] = result
        for dz in range(1, C):
            send(at(xsum.at[b], (z + dz) % C, ch), zrecv.at[b, dz], q_sem.at[b, dz], plane_peer(dz))

    def block(b, column, side, plane):
        first = b * W + side * part + plane * ch
        return qfull.at[column, pl.ds(pl.multiple_of(first, 8), ch)]

    def block_part(b, column, side):
        return qfull.at[column, pl.ds(pl.multiple_of(b * W + side * part, 8), part)]

    def plane_in(b):
        result = xsum[b, pl.ds(pl.multiple_of(z * ch, 8), ch)]
        for dz in range(1, C):
            arrived(zrecv.at[b, dz], q_sem.at[b, dz])
            result = result + zrecv[b, dz]
        piece = block(b, c, i, z)
        piece[...] = result
        for dz in range(1, C):
            send(piece, piece, gz_sem.at[b, dz], plane_peer(dz))

    def gram_part(b, di, dc, base):
        return block_part(b, (base + C - dc) % C, (i + g - di) % g)

    def to_side(b, dc):
        piece = gram_part(b, 0, dc, c)
        for di in range(1, g):
            send(piece, piece, gx_sem.at[b, di, dc // 2], side_peer(di))

    def to_rows(b, di):
        piece = gram_part(b, di, 0, c)
        for dc in range(2, C, 2):
            send(piece, piece, gy_sem.at[b, di, dc // 2], (p, (c + dc) % C))

    def to_partner(b, di, dc):
        piece = gram_part(b, di, dc, c)
        send(piece, piece, gc_sem.at[b, di, dc // 2], (p, partner))

    def side_arrived(b, di, dc):
        arrived(gram_part(b, di, dc, c), gx_sem.at[b, di, dc // 2])

    def rows_arrived(b, di, dc):
        arrived(gram_part(b, di, dc, c), gy_sem.at[b, di, dc // 2])

    def gather_side(b):
        for dz in range(1, C):
            arrived(block(b, c, i, (z + C - dz) % C), gz_sem.at[b, dz])
        to_side(b, 0)
        to_rows(b, 0)
        to_partner(b, 0, 0)

    def gather_row(b):
        if b == 1:
            for dc in range(2, C, 2):
                rows_arrived(b, 0, dc)
                to_side(b, dc)
                to_partner(b, 0, dc)
        else:
            for di in range(1, g):
                side_arrived(b, di, 0)
                to_rows(b, di)
                to_partner(b, di, 0)

    def gather_core(b):
        if b == 1:
            for di in range(1, g):
                for dc in range(0, C, 2):
                    side_arrived(b, di, dc)
                    to_partner(b, di, dc)
        else:
            for di in range(g):
                for dc in range(2, C, 2):
                    rows_arrived(b, di, dc)
                    to_partner(b, di, dc)

    def gathered(b):
        for di in range(g):
            for dc in range(0, C, 2):
                piece = block_part(b, (partner + C - dc) % C, (i + g - di) % g)
                arrived(piece, gc_sem.at[b, di, dc // 2])

    for k in range(2):
        along(k, panels[k], z, 1)
        along(k, panels[k], z, -1)
        to_columns(k, panels[k], z)
    for k in range(2):
        for dz in range(1, C):
            for way in (1, -1):
                valid = (z >= dz) if way > 0 else (z + dz < C)
                plane = (z + C - way * dz) % C
                src, sem = zbuf.at[k, plane], z_sem.at[k, plane]
                pl.when(valid)(functools.partial(arrived, src, sem))
                if dz < C - 1:
                    along(k, src, plane, way, valid)
                to_columns(k, src, plane, valid)
        to_row(k)
        if k == 0:
            across(0)
            for copy in loads[2:]:
                copy.wait()
            x_pair = halves(x_v[...])
            row_one, row_two = live_column(list1, p * rows, rows), live_column(list2, p * rows, rows)
    row_onward(0)
    tile_product(0, list1)
    across(1)
    pair_sum(0)
    row_onward(1)
    row_arrived(0)
    left = halves(row_one * mrow[0])
    right_one = total(0, row_one)
    qbuf[0] = split_dot(left, right_one, FIRST)
    side_out(0)
    for copy in loads[:2]:
        copy.wait()
    for src, dst in ((l1_v, d1_out), (l2_v, d2_out)):
        pair = halves(src[...])
        dst[...] = split_dot(pair, pair, FIRST)
    tile_product(1, list2)
    pair_sum(1)
    row_arrived(1)
    left = halves(row_two * mrow[1])
    cross = split_dot(right_one, left, FIRST)
    for cc in range(C):
        qbuf[1, cc * wc:(cc + 1) * wc] = cross[:, cc * wc:(cc + 1) * wc]
    side_out(1)
    side_in(0)
    right_two = total(1, row_two)
    qbuf[2] = split_dot(left, right_two, FIRST)
    side_out(2)
    plane_in(0)
    side_in(1)
    gather_side(0)
    plane_in(1)
    side_in(2)
    gather_row(0)
    gather_side(1)
    plane_in(2)
    gather_core(0)
    gather_row(1)
    gather_side(2)
    rows_out(0)
    rows_out(1)
    gather_core(1)
    gather_row(2)

    u_pair = halves(u_v[...])
    gathered(0)
    for cc in range(C):
        d1_out[:, cc * wc:(cc + 1) * wc] += qfull[cc, 0:W]
    d1_u = split_dot(halves(d1_out[...]), u_pair, PLAIN)
    gather_core(2)
    for k in range(2):
        for dc in range(1, C):
            other = (c + dc) % C
            arrived(frow.at[k, other], f_sem.at[k, other])
    for cc in range(C):
        f_out[:, cc * wc:(cc + 1) * wc] = -frow[0, cc]
        s_out[:, cc * wc:(cc + 1) * wc] = frow[1, cc]
    f_u = split_dot(halves(f_out[...]), u_pair, PLAIN)
    s_out[...] = -live_column(list2, p * rows + c * span, span) * (f_u + s_out[...])

    gathered(1)
    for cc in range(C):
        for k in range(C):
            wt[cc * wc:(cc + 1) * wc, k * wc:(k + 1) * wc] = qfull[cc, W + k * wc:W + (k + 1) * wc]
    c_out[...] = wt[...] - d1_u
    d2_out[...] -= split_dot(u_pair, halves(c_out[...]), FIRST) + split_dot(
        halves(wt[...]), u_pair, FIRST
    )
    gathered(2)
    for cc in range(C):
        d2_out[:, cc * wc:(cc + 1) * wc] += qfull[cc, 2 * W:3 * W]

    assert len(pending) <= nsend
    for copy, when in pending:
        if when is None:
            copy.wait_send()
        else:
            pl.when(when)(copy.wait_send)


def solution(mesh):
    R, C = mesh.shape["prow"], mesh.shape["pcol"]
    g = R // C

    def local(inverse_pool, panel_one, panel_two, upper_two, lower_one, lower_two, list_one, list_two):
        span, W = panel_one.shape
        rows, K = inverse_pool.shape
        wc, half = W // C, C // 2
        panel = 2 * (C - 1) + (2 * C - 1) * g + 2 * (half - 1) * (g - 1) + half + (half - 1)
        reduced = half + (half - 1) + (C - 1)
        gram = (g - 1) + 2 * (C - 1) + (g - 1) + g * half + g * (half - 1)
        nsend = 2 * panel + 2 * reduced + 3 * gram
        f32, dma = jnp.float32, pltpu.SemaphoreType.DMA
        shapes = ((span, W), (W, W), (span, W), (W, W), (W, W))
        results = pl.pallas_call(
            functools.partial(body, R, C, nsend),
            out_shape=tuple(pltpu.VMEM(shape, f32) for shape in shapes),
            in_specs=[pl.BlockSpec(memory_space=pl.ANY)] * 6
            + [pl.BlockSpec(memory_space=pltpu.SMEM)] * 2,
            out_specs=(pl.BlockSpec(memory_space=pltpu.VMEM),) * 5,
            scratch_shapes=[
                pltpu.VMEM((rows, K), f32),
                pltpu.VMEM((W, W), f32),
                pltpu.VMEM((W, W), f32),
                pltpu.VMEM((W, W), f32),
                pltpu.VMEM((2, C, span, W), f32),
                pltpu.VMEM((2, K, W), f32),
                pltpu.VMEM((2, rows, W), f32),
                pltpu.VMEM((2, C, rows, wc), f32),
                pltpu.VMEM((2, half, rows, wc), f32),
                pltpu.VMEM((2, half, rows, wc), f32),
                pltpu.VMEM((2, rows, wc), f32),
                pltpu.VMEM((2, C, span, wc), f32),
                pltpu.VMEM((3, W, wc), f32),
                pltpu.VMEM((3, g, W // g, wc), f32),
                pltpu.VMEM((3, W // g, wc), f32),
                pltpu.VMEM((3, C, W // R, wc), f32),
                pltpu.VMEM((C, 3 * W, wc), f32),
                pltpu.VMEM((W, W), f32),
                dma((4,)),
                dma((nsend,)),
                dma((2, C)),
                dma((2, g * C)),
                dma((2, C)),
                dma((2, half)),
                dma((2, half)),
                dma((2, C)),
                dma((3, g)),
                dma((3, C)),
                dma((3, C)),
                dma((3, g, half)),
                dma((3, g, half)),
                dma((3, g, half)),
            ],
            compiler_params=pltpu.CompilerParams(collective_id=0, has_side_effects=True),
        )(inverse_pool, panel_one, panel_two, upper_two, lower_one, lower_two, list_one, list_two)
        return pl.pallas_call(
            write_out,
            out_shape=tuple(jax.ShapeDtypeStruct(shape, f32) for shape in shapes),
            in_specs=[pl.BlockSpec(memory_space=pl.ANY)] * 5,
            out_specs=(pl.BlockSpec(memory_space=pl.ANY),) * 5,
            scratch_shapes=[dma((5,))],
            compiler_params=pltpu.CompilerParams(vmem_limit_bytes=8 * W * W * 4),
        )(*results)

    return jax.shard_map(
        local,
        mesh=mesh,
        in_specs=(
            P("prow", "pcol"),
            P(("prow", "pcol"), None),
            P(("prow", "pcol"), None),
            P(),
            P(),
            P(),
            P(),
            P(),
        ),
        out_specs=(P(("prow", "pcol"), None), P(), P(("prow", "pcol"), None), P(), P()),
        check_vma=False,
    )
```
